32 devices in a mesh: wide: 8 (over z, x), narrow: 4 (over y, core).
Axes of the slice: x: 2, y: 2, z: 4, core: 2. Of those that a mesh axis runs over, the one named last changes fastest.
Arguments:
- fine_in: bfloat16 [16, 16, 64, 512], P(None, None, 'wide', 'narrow'), may hold values from -6 to 6
- coarse_in: bfloat16 [64, 16, 16, 128], P(None, 'wide', 'narrow'), may hold values from -6 to 6
- w_fine1: bfloat16 [16, 16, 3, 3, 3], replicated, may hold values from -0.3125 to 0.3125
- b_fine1: float32 [16], replicated, may hold values from -3 to 3
- w_fine2: bfloat16 [16, 16, 3, 3, 3], replicated, may hold values from -0.3125 to 0.3125
- b_fine2: float32 [16], replicated, may hold values from -3 to 3
- w_coarse1: bfloat16 [64, 80, 3, 3, 3], replicated, may hold values from -0.125 to 0.125
- b_coarse1: float32 [64], replicated, may hold values from -3 to 3
- w_coarse2: bfloat16 [64, 64, 3, 3, 3], replicated, may hold values from -0.15625 to 0.15625
- b_coarse2: float32 [64], replicated, may hold values from -3 to 3
- w_proj: bfloat16 [16, 64], replicated, may hold values from -0.75 to 0.75
Outputs:
- fine_out: bfloat16 [16, 16, 64, 512], P(None, None, 'wide', 'narrow')
- coarse_out: bfloat16 [64, 16, 16, 128], P(None, 'wide', 'narrow')
The draws below stay inside these ranges and needn't reach their ends.
All inputs are finite; a program needn't handle non-finite values.
Results may differ from the reference program's by a relative error of at most 0.0075.
Values may be sent and summed in bfloat16 or wider, within the bound.
A program may use at most 192 MiB of HBM per device.

```python
import jax
import jax.numpy as jnp
from jax import lax

CF = 16
CC = 64
Z = 16
FY = 64
FX = 512
CY = 16
CX = 128


def levels(own_key, dims, pieces, smallest, high):
    def one(dim, parts):
        draws = jax.random.uniform(jax.random.fold_in(jax.random.fold_in(own_key, 6), dim), (parts,), jnp.float32, smallest / len(pieces), high / len(pieces))
        return jnp.repeat(jnp.exp(draws), dims[dim] // parts).reshape((-1,) + (1,) * (len(dims) - dim - 1))

    loudness = one(*pieces[0])
    for cut in pieces[1:]:
        loudness = loudness * one(*cut)
    return loudness


def normal_values(rng, dims, width, bound, split=(), dtype=jnp.bfloat16):
    values = width * jax.random.normal(rng, dims, jnp.float32)
    if split:
        values = values * levels(rng, dims, split, -0.22, 0.18)
    return jnp.clip(values, -bound, bound).astype(dtype)


def setup_inputs(seed: int = 0) -> dict:
    streams_of = jax.random.split(jax.random.key(seed), 12)
    fine_in = normal_values(streams_of[0], (CF, Z, FY, FX), 1.0, 6.0, ((2, 8), (3, 4)))
    coarse_in = normal_values(streams_of[1], (CC, Z, CY, CX), 1.0, 6.0, ((1, 8), (2, 4)))
    w_fine1 = normal_values(streams_of[2], (CF, CF, 3, 3, 3), (CF * 27) ** -0.5, 0.3125)
    b_fine1 = normal_values(streams_of[3], (CF,), 0.5, 3.0, (), jnp.float32)
    w_fine2 = normal_values(streams_of[4], (CF, CF, 3, 3, 3), (CF * 27) ** -0.5, 0.3125)
    b_fine2 = normal_values(streams_of[5], (CF,), 0.5, 3.0, (), jnp.float32)
    w_coarse1 = normal_values(streams_of[6], (CC, CC + CF, 3, 3, 3), ((CC + CF) * 27) ** -0.5, 0.125)
    b_coarse1 = normal_values(streams_of[7], (CC,), 0.5, 3.0, (), jnp.float32)
    w_coarse2 = normal_values(streams_of[8], (CC, CC, 3, 3, 3), (CC * 27) ** -0.5, 0.15625)
    b_coarse2 = normal_values(streams_of[9], (CC,), 0.5, 3.0, (), jnp.float32)
    w_proj = normal_values(streams_of[10], (CF, CC), CC ** -0.5, 0.75)
    return {"fine_in": fine_in, "coarse_in": coarse_in, "w_fine1": w_fine1, "b_fine1": b_fine1, "w_fine2": w_fine2, "b_fine2": b_fine2, "w_coarse1": w_coarse1, "b_coarse1": b_coarse1, "w_coarse2": w_coarse2, "b_coarse2": b_coarse2, "w_proj": w_proj}


def convolve(field, kernel, offset):
    result = lax.conv_general_dilated(field.astype(jnp.float32)[None], kernel.astype(jnp.float32), (1, 1, 1), ((1, 1), (1, 1), (1, 1)), dimension_numbers=("NCDHW", "OIDHW", "NCDHW"), preferred_element_type=jnp.float32)[0]
    return result + offset[:, None, None, None]


def reference(fine_in, coarse_in, w_fine1, b_fine1, w_fine2, b_fine2, w_coarse1, b_coarse1, w_coarse2, b_coarse2, w_proj):
    hidden = jnp.maximum(convolve(fine_in, w_fine1, b_fine1), 0.0).astype(jnp.bfloat16)
    pooled = hidden.astype(jnp.float32).reshape(CF, Z, CY, 4, CX, 4).mean(axis=(3, 5)).astype(jnp.bfloat16)
    stacked = jnp.concatenate([coarse_in, pooled], axis=0)
    coarse_mid = jnp.maximum(convolve(stacked, w_coarse1, b_coarse1), 0.0).astype(jnp.bfloat16)
    coarse_out = jnp.maximum(convolve(coarse_mid, w_coarse2, b_coarse2), 0.0).astype(jnp.bfloat16)
    context = jnp.einsum("fc,czyx->fzyx", w_proj.astype(jnp.float32), coarse_out.astype(jnp.float32)).astype(jnp.bfloat16)
    fine_term = convolve(hidden, w_fine2, b_fine2)
    widened = jnp.broadcast_to(context[:, :, :, None, :, None], (CF, Z, CY, 4, CX, 4)).reshape(CF, Z, FY, FX)
    fine_out = (fine_term + widened.astype(jnp.float32)).astype(jnp.bfloat16)
    return fine_out, coarse_out
```

```python
import functools

import jax
import jax.numpy as jnp
from jax import lax
from jax.experimental import pallas as pl
from jax.experimental.pallas import tpu as pltpu
from jax.sharding import PartitionSpec as P

F32, BF16 = jnp.float32, jnp.bfloat16


def dot(a, b):
    return jnp.dot(a, b, preferred_element_type=F32)


def lanes(shape):
    return lax.broadcasted_iota(jnp.int32, shape, len(shape) - 1)


def kernel(
    dims,
    fine, coarse, k1, k2, kc, kp, km, b1, b2, bc1, bc2, wp,
    out, cout,
    halo1, edge1, side1, halo2, edge2, side2, band, x3, hidden,
    cbuf, pool, prcv, xc3, xp3, wc, wq, x3m, wm, ctx, crcv,
    fsend, frecv, hsend, hrecv, csend, crecv, psend, precv, tsend, trecv, lsem,
):
    nw, nn, depth, cf, cc, fy, cz, cy, cx, xs = dims
    rows, crow = depth * cf, cz * cc
    reach = cy // 2
    w, n = lax.axis_index("wide"), lax.axis_index("narrow")

    def at(a, b):
        return {"wide": a, "narrow": b}

    barrier = pltpu.get_barrier_semaphore()

    def greet(i, carry):
        a, b = i // nn, i % nn

        @pl.when(jnp.logical_or(a != w, b != n))
        def _():
            pl.semaphore_signal(barrier, inc=1, device_id=at(a, b))

        return carry

    lax.fori_loop(0, nw * nn, greet, 0)

    def remote(src, dst, ssem, rsem, a, b):
        return pltpu.make_async_remote_copy(
            src_ref=src, dst_ref=dst, send_sem=ssem, recv_sem=rsem,
            device_id=at(a, b), device_id_type=pl.DeviceIdType.MESH)

    def inside(a, b):
        ok_a = jnp.logical_and(a >= 0, a < nw)
        ok_b = jnp.logical_and(b >= 0, b < nn)
        return jnp.logical_and(ok_a, ok_b)

    lane = lanes((rows, cx))

    def pack(row_of, edge):
        total = jnp.zeros((rows, cx), F32)
        for y in range(fy):
            row = row_of(y).astype(F32)
            first = pltpu.roll(row, y, 1) if y else row
            total = jnp.where(lane == y, first, total)
            total = jnp.where(lane == 64 + y, pltpu.roll(row, 65 + y, 1), total)
        edge[...] = total.astype(BF16)

    around = ((-1, 0), (1, 0), (0, -1), (0, 1), (-1, -1), (-1, 1), (1, -1), (1, 1))

    def fine_copies(top, bottom, edge, halo, side, ssem, rsem):
        made = []
        for i, (da, db) in enumerate(around):
            if i == 0:
                src, dst = bottom, halo.at[0]
            elif i == 1:
                src, dst = top, halo.at[1]
            else:
                src, dst = edge, side.at[i - 2]
            made.append((dst, w - da, n - db, w + da, n + db,
                         remote(src, dst, ssem.at[i], rsem.at[i], w - da, n - db)))
        return made

    def send(made):
        for dst, a, b, _, _, copy in made:
            pl.when(inside(a, b))(copy.start)

    def clear(made):
        for dst, _, _, a, b, copy in made:
            @pl.when(jnp.logical_not(inside(a, b)))
            def _(dst=dst):
                dst[...] = jnp.zeros(dst.shape, BF16)

    def receive(made):
        for dst, _, _, a, b, copy in made:
            pl.when(inside(a, b))(copy.wait_recv)

    def sent(made):
        for dst, a, b, _, _, copy in made:
            pl.when(inside(a, b))(copy.wait_send)

    def expand(row_of, halo, side):
        left, right, ul, ur, dl, dr = [side[i].astype(F32) for i in range(6)]
        for y in range(-1, fy + 1):
            if y < 0:
                raw, lcol, rcol, j = halo[0], ul, ur, fy - 1
            elif y == fy:
                raw, lcol, rcol, j = halo[1], dl, dr, 0
            else:
                raw, lcol, rcol, j = row_of(y), left, right, y
            row = raw.astype(F32)
            cols = pl.ds((y + 1) * cx, cx)
            x3[pl.ds(rows, rows), cols] = raw
            x3[pl.ds(0, rows), cols] = jnp.where(
                lane == 0, pltpu.roll(lcol, 64 - j, 1), pltpu.roll(row, 1, 1)).astype(BF16)
            moved = pltpu.roll(rcol, cx - 1 - j, 1)
            x3[pl.ds(2 * rows, rows), cols] = jnp.where(
                lane == cx - 1, moved, pltpu.roll(row, cx - 1, 1)).astype(BF16)

    def bands(base):
        spot = lanes((cf, rows))
        for tap in range(9):
            dy, dx = tap // 3, tap % 3
            piece = base[tap]
            for z in range(depth):
                part = pltpu.roll(piece, z * cf, 1) if z else piece
                if z == 0:
                    part = jnp.where(spot >= rows - cf, 0.0, part)
                if z == depth - 1:
                    part = jnp.where(spot < cf, 0.0, part)
                band[dy, pl.ds(z * cf, cf), pl.ds(dx * rows, rows)] = part.astype(BF16)

    def short_bands(base, target, count, step):
        size, width = base.shape[1], base.shape[2]
        for tap in range(9):
            dy, dx = tap // 3, tap % 3
            piece = base[tap]
            for z in range(count):
                part = pltpu.roll(piece, z * step, 1) if z else piece
                target[dy, pl.ds(z * size, size), pl.ds(dx * width, width)] = part.astype(BF16)

    def conv(weights, field, start, width):
        total = None
        for dy in range(3):
            term = dot(weights[dy], field[:, pl.ds(start + dy * cx, width)])
            total = term if total is None else total + term
        return total

    pack(lambda y: fine[y], edge1)
    first = fine_copies(fine.at[0], fine.at[fy - 1], edge1, halo1, side1, fsend, frecv)
    cmade = []
    for i, (da, db) in enumerate(around):
        zpos = pl.ds((da + 1) * crow, crow)
        if db == 0:
            src, dst = coarse, cbuf.at[pl.ds(2, cy), zpos]
        elif db < 0:
            src, dst = coarse.at[pl.ds(cy - 2, 2)], cbuf.at[pl.ds(0, 2), zpos]
        else:
            src, dst = coarse.at[pl.ds(0, 2)], cbuf.at[pl.ds(cy + 2, 2), zpos]
        cmade.append((dst, w - da, n - db, w + da, n + db,
                      remote(src, dst, csend.at[i], crecv.at[i], w - da, n - db)))
    pl.semaphore_wait(barrier, nw * nn - 1)
    send(first)
    send(cmade)
    clear(first)
    clear(cmade)
    cbuf[pl.ds(2, cy), pl.ds(crow, crow), :] = coarse[...]
    pool[pl.ds(0, 2 * cf), :] = jnp.zeros((2 * cf, cx), BF16)
    pool[pl.ds(2 * cf + rows, 2 * cf), :] = jnp.zeros((2 * cf, cx), BF16)
    bands(k1)
    receive(first)
    expand(lambda y: fine[y], halo1, side1)

    source = lax.broadcasted_iota(jnp.int32, (cx, cx), 0)
    target = lanes((cx, cx))
    for g in range(fy // 4):
        place = jnp.where(target == source // 4 + g * xs, 1.0, 0.0).astype(BF16)
        total = None
        for h in range(2):
            y = g * 4 + h * 2
            both = jnp.maximum(conv(band, x3, y * cx, 2 * cx) + b1[...], 0.0).astype(BF16)
            for k in range(2):
                row = both[:, k * cx:(k + 1) * cx]
                hidden[y + k] = row
                term = dot(row, place)
                total = term if total is None else total + term
        if g == 0:
            summed = total
        else:
            summed = summed + total
    pool[pl.ds(2 * cf, rows), :] = (summed * (1.0 / 16.0)).astype(BF16)

    tall = (cz + 4) * cf

    def pooled_copy(a, which, b):
        k = w - b * reach + 1
        return remote(pool.at[pl.ds(pl.multiple_of(a * cz * cf, cf), tall)], prcv.at[k, n],
                      psend.at[which, a], precv.at[k, n], a, b)

    def local_copy():
        k = w - n * reach + 1
        return pltpu.make_async_copy(pool.at[pl.ds(pl.multiple_of(w * cz * cf, cf), tall)],
                                     prcv.at[k, n], precv.at[k, n])

    home = w // reach
    rest = w % reach
    targets = (
        (home, None),
        (home - 1, jnp.logical_and(rest == 0, home >= 1)),
        (home + 1, jnp.logical_and(rest == reach - 1, home + 1 < nn)),
    )

    def each_target(start):
        for which, (b, ok) in enumerate(targets):
            def step(a, carry, which=which, b=b, ok=ok):
                self_ = jnp.logical_and(a == w, b == n)
                go = jnp.logical_not(self_)
                if ok is not None:
                    go = jnp.logical_and(go, ok)

                @pl.when(go)
                def _():
                    copy = pooled_copy(a, which, b)
                    if start:
                        copy.start()
                    else:
                        copy.wait_send()

                if start:
                    mine = self_ if ok is None else jnp.logical_and(self_, ok)

                    @pl.when(mine)
                    def _():
                        local_copy().start()

                return carry

            lax.fori_loop(0, nw, step, 0)

    each_target(True)
    pack(lambda y: hidden[y], edge2)
    second = fine_copies(hidden.at[0], hidden.at[fy - 1], edge2, halo2, side2, hsend, hrecv)
    send(second)
    clear(second)

    short_bands(kc, wc, cz + 2, cc)
    short_bands(kp, wq, cz + 2, cf)
    short_bands(km, wm, cz, cc)
    receive(cmade)

    def spread(field, raw, y, height):
        row = raw.astype(F32)
        spot = lanes(row.shape)
        cols = pl.ds(y * cx, cx)
        field[pl.ds(height, raw.shape[0]), cols] = raw
        field[pl.ds(0, raw.shape[0]), cols] = jnp.where(
            spot == 0, 0.0, pltpu.roll(row, 1, 1)).astype(BF16)
        field[pl.ds(2 * height, raw.shape[0]), cols] = jnp.where(
            spot == cx - 1, 0.0, pltpu.roll(row, cx - 1, 1)).astype(BF16)

    for y in range(cy + 4):
        spread(xc3, cbuf[y], y, (cz + 4) * cc)
    high = wq.shape[2] // 3
    if high > tall:
        for dx in range(3):
            xp3[pl.ds(dx * high + tall, high - tall), :] = jnp.zeros(
                (high - tall, xp3.shape[1]), BF16)
    lowl = lax.broadcasted_iota(jnp.int32, (cx, 2 * cx), 0)
    wide_ = lanes((cx, 2 * cx))
    for k in range(reach + 2):
        tile = n * reach + k - 1
        ok = jnp.logical_and(tile >= 0, tile < nw)

        @pl.when(ok)
        def _(k=k):
            total = None
            for m in range(nn):
                pltpu.make_async_copy(pool.at[pl.ds(0, tall)], prcv.at[k, m], precv.at[k, m]).wait()
                goal = (lowl // xs) * cx + m * xs + lowl % xs
                keep = jnp.logical_and(goal == wide_, lowl < 2 * xs)
                term = dot(prcv[k, m], jnp.where(keep, 1.0, 0.0).astype(BF16))
                total = term if total is None else total + term
            both = total.astype(BF16)
            for j in range(2):
                spread(xp3, both[:, j * cx:(j + 1) * cx], 2 * k + j, high)

        @pl.when(jnp.logical_not(ok))
        def _(k=k):
            for dx in range(3):
                xp3[pl.ds(dx * high, tall), pl.ds(2 * k * cx, 2 * cx)] = jnp.zeros(
                    (tall, 2 * cx), BF16)

    mids = (cz + 2) * cc
    zrow = lax.broadcasted_iota(jnp.int32, (mids, 1), 0) // cc + (w * cz - 1)
    zok = jnp.logical_and(zrow >= 0, zrow < nw * cz)
    for h in range((cy + 2) // 2):
        both = conv(wc, xc3, 2 * h * cx, 2 * cx) + conv(wq, xp3, 2 * h * cx, 2 * cx)
        both = jnp.maximum(both + bc1[...], 0.0)
        ypos = lanes((mids, 2 * cx)) // cx + (n * cy - 1 + 2 * h)
        yok = jnp.logical_and(ypos >= 0, ypos < nn * cy)
        both = jnp.where(jnp.logical_and(zok, yok), both, 0.0).astype(BF16)
        for j in range(2):
            spread(x3m, both[:, j * cx:(j + 1) * cx], 2 * h + j, mids)
    for h in range(cy // 2):
        both = jnp.maximum(conv(wm, x3m, 2 * h * cx, 2 * cx) + bc2[...], 0.0).astype(BF16)
        near = dot(wp[...], both).astype(BF16)
        for j in range(2):
            cout[2 * h + j] = both[:, j * cx:(j + 1) * cx]
            ctx[2 * h + j] = near[:, j * cx:(j + 1) * cx]

    slab = cz * cf

    def context_copy(k, m):
        return remote(ctx.at[pl.ds(2 * k, 2)],
                      crcv.at[:, pl.ds(pl.multiple_of(w * slab, slab), slab)],
                      tsend.at[k, m], trecv.at[w], n * reach + k, m)

    def context_step(start):
        def step(i, carry):
            k, m = i // nn, i % nn
            self_ = jnp.logical_and(n * reach + k == w, m == n)

            @pl.when(jnp.logical_not(self_))
            def _():
                copy = context_copy(k, m)
                if start:
                    copy.start()
                else:
                    copy.wait_send()

            if start:
                @pl.when(self_)
                def _():
                    pltpu.make_async_copy(
                        ctx.at[pl.ds(2 * k, 2)],
                        crcv.at[:, pl.ds(pl.multiple_of(w * slab, slab), slab)],
                        trecv.at[w]).start()

            return carry

        lax.fori_loop(0, reach * nn, step, 0)

    context_step(True)
    bands(k2)
    receive(second)
    expand(lambda y: hidden[y], halo2, side2)
    for a in range(nw):
        pltpu.make_async_copy(ctx.at[pl.ds(0, 2)], crcv.at[:, pl.ds(a * slab, slab)],
                              trecv.at[a]).wait()
    grow = jnp.where(source == target // 4 + n * xs, 1.0, 0.0).astype(BF16)
    for g in range(fy // 4):
        more = dot(crcv[g], grow) + b2[...]
        for h in range(2):
            y = g * 4 + h * 2
            both = conv(band, x3, y * cx, 2 * cx)
            for k in range(2):
                out[y + k] = (both[:, k * cx:(k + 1) * cx] + more).astype(BF16)

    sent(first)
    sent(cmade)
    sent(second)
    each_target(False)
    context_step(False)


def local(fine_in, coarse_in, w1, b1, w2, b2, wc1, bc1, wc2, bc2, w_proj):
    nw, nn = lax.axis_size("wide"), lax.axis_size("narrow")
    cf, depth, fy, fx = fine_in.shape
    cc, cz, cy, cx = coarse_in.shape
    xs = fx // 4
    rows, crow, reach = depth * cf, cz * cc, cy // 2
    fine = fine_in.transpose(2, 1, 0, 3).reshape(fy, rows, fx)
    coarse = coarse_in.transpose(2, 1, 0, 3).reshape(cy, crow, cx)

    def base(kernel):
        o, i = kernel.shape[:2]
        return kernel.transpose(3, 4, 0, 2, 1).reshape(9, o, 3 * i).astype(F32)

    def fine_base(kernel):
        flat = base(kernel)
        gap = jnp.zeros((9, cf, rows - 3 * cf), F32)
        return jnp.concatenate([flat[:, :, cf:], gap, flat[:, :, :cf]], axis=2)

    def widened(kernel, width):
        flat = base(kernel)
        return jnp.pad(flat, ((0, 0), (0, 0), (0, width - flat.shape[2])))

    high = -(-(cz + 4) * cf // 128) * 128
    mids = (cz + 2) * cc
    tall = (cz + 4) * cf
    args = (
        fine, coarse, fine_base(w1), fine_base(w2),
        widened(wc1[:, :cc], (cz + 4) * cc), widened(wc1[:, cc:], high), widened(wc2, mids),
        jnp.tile(b1, depth)[:, None], jnp.tile(b2, depth)[:, None],
        jnp.tile(bc1, cz + 2)[:, None], jnp.tile(bc2, cz)[:, None],
        jnp.einsum("fc,pq->pfqc", w_proj, jnp.eye(cz, dtype=BF16)).reshape(cz * cf, crow),
    )
    dims = (nw, nn, depth, cf, cc, fy, cz, cy, cx, xs)
    dma = pltpu.SemaphoreType.DMA
    vmem = pltpu.VMEM
    out, cout = pl.pallas_call(
        functools.partial(kernel, dims),
        name="unet",
        out_shape=(
            jax.ShapeDtypeStruct((fy, rows, fx), BF16),
            jax.ShapeDtypeStruct((cy, crow, cx), BF16),
        ),
        in_specs=[pl.BlockSpec(memory_space=pltpu.VMEM)] * len(args),
        out_specs=(pl.BlockSpec(memory_space=pltpu.VMEM),) * 2,
        scratch_shapes=[
            vmem((2, rows, cx), BF16), vmem((rows, cx), BF16), vmem((6, rows, cx), BF16),
            vmem((2, rows, cx), BF16), vmem((rows, cx), BF16), vmem((6, rows, cx), BF16),
            vmem((3, rows, 3 * rows), BF16), vmem((3 * rows, (fy + 2) * cx), BF16),
            vmem((fy, rows, cx), BF16),
            vmem((cy + 4, 3 * crow, cx), BF16), vmem((rows + 4 * cf, cx), BF16),
            vmem((reach + 2, nn, tall, cx), BF16),
            vmem((3 * 3 * crow, (cy + 4) * cx), BF16), vmem((3 * high, (cy + 4) * cx), BF16),
            vmem((3, mids, 9 * crow), BF16), vmem((3, mids, 3 * high), BF16),
            vmem((3 * mids, (cy + 2) * cx), BF16), vmem((3, crow, 3 * mids), BF16),
            vmem((cy, cz * cf, cx), BF16), vmem((2, rows, cx), BF16),
            dma((8,)), dma((8,)), dma((8,)), dma((8,)), dma((8,)), dma((8,)),
            dma((3, nw)), dma((reach + 2, nn)), dma((reach, nn)), dma((nw,)), dma,
        ],
        compiler_params=pltpu.CompilerParams(
            collective_id=0, has_side_effects=True, vmem_limit_bytes=63 << 20),
    )(*args)
    fine_out = out.reshape(fy, depth, cf, fx).transpose(2, 1, 0, 3)
    coarse_out = cout.reshape(cy, cz, cc, cx).transpose(2, 1, 0, 3)
    return fine_out, coarse_out


def solution(mesh):
    return jax.shard_map(
        local,
        mesh=mesh,
        in_specs=(
            P(None, None, "wide", "narrow"),
            P(None, "wide", "narrow", None),
        ) + (P(),) * 9,
        out_specs=(P(None, None, "wide", "narrow"), P(None, "wide", "narrow", None)),
        check_vma=False,
    )
```

```python
import functools

import jax
import jax.numpy as jnp
from jax import lax
from jax.experimental import pallas as pl
from jax.experimental.pallas import tpu as pltpu
from jax.sharding import PartitionSpec as P

F32, BF16 = jnp.float32, jnp.bfloat16


def dot(a, b):
    return jnp.dot(a, b, preferred_element_type=F32)


def lanes(shape):
    return lax.broadcasted_iota(jnp.int32, shape, len(shape) - 1)


def kernel(
    dims,
    fine, coarse, k1, k2, k3, k4, b1_, b2_, bc1_, bc2_, wp,
    out, cout,
    halo1, edge1, side1, halo2, edge2, side2, band, x3, hidden,
    cbuf, pool, prcv, xc3, xp3, wc, wq, x3m, wm, ctx, crcv,
    fsend, frecv, hsend, hrecv, csend, crecv, psend, precv, tsend, trecv, lsem,
):
    nw, nn, depth, cf, cc, fy, cz, cy, cx, xs = dims
    rows, crow = depth * cf, cz * cc
    reach = cy // 2
    w, n = lax.axis_index("wide"), lax.axis_index("narrow")

    def at(a, b):
        return {"wide": a, "narrow": b}

    barrier = pltpu.get_barrier_semaphore()

    def greet(i, carry):
        a, b = i // nn, i % nn

        @pl.when(jnp.logical_or(a != w, b != n))
        def _():
            pl.semaphore_signal(barrier, inc=1, device_id=at(a, b))

        return carry

    lax.fori_loop(0, nw * nn, greet, 0)

    def remote(src, dst, ssem, rsem, a, b):
        return pltpu.make_async_remote_copy(
            src_ref=src, dst_ref=dst, send_sem=ssem, recv_sem=rsem,
            device_id=at(a, b), device_id_type=pl.DeviceIdType.MESH)

    def inside(a, b):
        ok_a = jnp.logical_and(a >= 0, a < nw)
        ok_b = jnp.logical_and(b >= 0, b < nn)
        return jnp.logical_and(ok_a, ok_b)

    lane = lanes((rows, cx))

    def column(bias, copies):
        size = bias.shape[1]
        square = jnp.broadcast_to(bias[...], (size, size))
        diagonal = lax.broadcasted_iota(jnp.int32, (size, size), 0) == lanes((size, size))
        one = jnp.sum(jnp.where(diagonal, square, 0.0), axis=1, keepdims=True)
        return jnp.concatenate([one] * copies, axis=0)

    b1, b2 = column(b1_, depth), column(b2_, depth)
    bc1, bc2 = column(bc1_, cz + 2), column(bc2_, cz)

    def taps(weights, tap, start, size, width, wrap):
        parts = [weights[dz * 9 + tap][:, start:start + size].astype(F32) for dz in range(3)]
        gap = jnp.zeros((parts[0].shape[0], width - 3 * size), F32)
        if wrap:
            return jnp.concatenate([parts[1], parts[2], gap, parts[0]], axis=1)
        return jnp.concatenate(parts + [gap], axis=1)

    def pack(row_of, edge):
        total = jnp.zeros((rows, cx), F32)
        for y in range(fy):
            row = row_of(y).astype(F32)
            first = pltpu.roll(row, y, 1) if y else row
            total = jnp.where(lane == y, first, total)
            last = pltpu.roll(row, fy + 1 + y, 1)
            total = jnp.where(lane == fy + y, last, total)
        edge[...] = total.T[:2 * fy].astype(BF16)

    around = ((-1, 0), (1, 0), (0, -1), (0, 1), (-1, -1), (-1, 1), (1, -1), (1, 1))

    def fine_copies(top, bottom, edge, halo, side, ssem, rsem):
        made = []
        for i, (da, db) in enumerate(around):
            if i == 0:
                src, dst = bottom, halo.at[0]
            elif i == 1:
                src, dst = top, halo.at[1]
            else:
                src, dst = edge, side.at[i - 2]
            made.append((dst, w - da, n - db, w + da, n + db,
                         remote(src, dst, ssem.at[i], rsem.at[i], w - da, n - db)))
        return made

    def send(made):
        for dst, a, b, _, _, copy in made:
            pl.when(inside(a, b))(copy.start)

    def clear(made):
        for dst, _, _, a, b, copy in made:
            @pl.when(jnp.logical_not(inside(a, b)))
            def _(dst=dst):
                dst[...] = jnp.zeros(dst.shape, BF16)

    def receive(made):
        for dst, _, _, a, b, copy in made:
            pl.when(inside(a, b))(copy.wait_recv)

    def sent(made):
        for dst, a, b, _, _, copy in made:
            pl.when(inside(a, b))(copy.wait_send)

    def expand(row_of, halo, side):
        gap = jnp.zeros((cx - 2 * fy, rows), F32)
        left, right, ul, ur, dl, dr = [
            jnp.concatenate([side[i].astype(F32), gap], axis=0).T for i in range(6)]
        for y in range(-1, fy + 1):
            if y < 0:
                raw, lcol, rcol, j = halo[0], ul, ur, fy - 1
            elif y == fy:
                raw, lcol, rcol, j = halo[1], dl, dr, 0
            else:
                raw, lcol, rcol, j = row_of(y), left, right, y
            row = raw.astype(F32)
            cols = pl.ds((y + 1) * cx, cx)
            x3[pl.ds(rows, rows), cols] = raw
            x3[pl.ds(0, rows), cols] = jnp.where(
                lane == 0, pltpu.roll(lcol, cx - fy - j, 1), pltpu.roll(row, 1, 1)).astype(BF16)
            moved = pltpu.roll(rcol, cx - 1 - j, 1)
            x3[pl.ds(2 * rows, rows), cols] = jnp.where(
                lane == cx - 1, moved, pltpu.roll(row, cx - 1, 1)).astype(BF16)

    def bands(base):
        spot = lanes((cf, rows))
        for tap in range(9):
            dy, dx = tap // 3, tap % 3
            piece = taps(base, tap, 0, cf, rows, True)
            for z in range(depth):
                part = pltpu.roll(piece, z * cf, 1) if z else piece
                if z == 0:
                    part = jnp.where(spot >= rows - cf, 0.0, part)
                if z == depth - 1:
                    part = jnp.where(spot < cf, 0.0, part)
                band[dy, pl.ds(z * cf, cf), pl.ds(dx * rows, rows)] = part.astype(BF16)

    def short_bands(base, target, count, start, step):
        size, width = base.shape[1], target.shape[2] // 3
        for tap in range(9):
            dy, dx = tap // 3, tap % 3
            piece = taps(base, tap, start, step, width, False)
            for z in range(count):
                part = pltpu.roll(piece, z * step, 1) if z else piece
                target[dy, pl.ds(z * size, size), pl.ds(dx * width, width)] = part.astype(BF16)

    def conv(weights, field, start, width):
        total = None
        for dy in range(3):
            term = dot(weights[dy], field[:, pl.ds(start + dy * cx, width)])
            total = term if total is None else total + term
        return total

    pack(lambda y: fine[y], edge1)
    first = fine_copies(fine.at[0], fine.at[fy - 1], edge1, halo1, side1, fsend, frecv)
    cmade = []
    for i, (da, db) in enumerate(around):
        zpos = pl.ds((da + 1) * crow, crow)
        if db == 0:
            src, dst = coarse, cbuf.at[pl.ds(2, cy), zpos]
        elif db < 0:
            src, dst = coarse.at[pl.ds(cy - 2, 2)], cbuf.at[pl.ds(0, 2), zpos]
        else:
            src, dst = coarse.at[pl.ds(0, 2)], cbuf.at[pl.ds(cy + 2, 2), zpos]
        cmade.append((dst, w - da, n - db, w + da, n + db,
                      remote(src, dst, csend.at[i], crecv.at[i], w - da, n - db)))
    pl.semaphore_wait(barrier, nw * nn - 1)
    send(first)
    clear(first)
    clear(cmade)
    cbuf[pl.ds(2, cy), pl.ds(crow, crow), :] = coarse[...]
    pool[pl.ds(0, cf), :] = jnp.zeros((cf, cx), BF16)
    pool[pl.ds(cf + rows // 2, cf), :] = jnp.zeros((cf, cx), BF16)
    bands(k1)
    receive(first)
    send(cmade)
    expand(lambda y: fine[y], halo1, side1)

    source = lax.broadcasted_iota(jnp.int32, (cx, cx), 0)
    target = lanes((cx, cx))
    for g in range(fy // 4):
        place = jnp.where(target == source // 4 + g * xs, 1.0, 0.0).astype(BF16)
        total = None
        for h in range(2):
            y = g * 4 + h * 2
            both = jnp.maximum(conv(band, x3, y * cx, 2 * cx) + b1, 0.0).astype(BF16)
            for k in range(2):
                row = both[:, k * cx:(k + 1) * cx]
                hidden[y + k] = row
                term = dot(row, place)
                total = term if total is None else total + term
        if g == 0:
            summed = total
        else:
            summed = summed + total
    mean = summed * (1.0 / 16.0)
    turned = pltpu.roll(mean, cx // 2, 1)
    for z in range(depth // 2):
        first_z = mean[2 * z * cf:(2 * z + 1) * cf]
        pool[pl.ds((z + 1) * cf, cf), :] = (
            first_z + turned[(2 * z + 1) * cf:(2 * z + 2) * cf]).astype(BF16)

    tall = (cz + 4) * cf
    half = tall // 2
    step_z = cz // 2 * cf

    def pooled_copy(a, which, b):
        k = w - b * reach + 1
        return remote(pool.at[pl.ds(pl.multiple_of(a * step_z, cf), half)], prcv.at[k, n],
                      psend.at[which, a], precv.at[k, n], a, b)

    def local_copy():
        k = w - n * reach + 1
        return pltpu.make_async_copy(pool.at[pl.ds(pl.multiple_of(w * step_z, cf), half)],
                                     prcv.at[k, n], precv.at[k, n])

    home = w // reach
    rest = w % reach
    targets = (
        (home, None),
        (home - 1, jnp.logical_and(rest == 0, home >= 1)),
        (home + 1, jnp.logical_and(rest == reach - 1, home + 1 < nn)),
    )

    def each_target(start):
        for which, (b, ok) in enumerate(targets):
            def step(a, carry, which=which, b=b, ok=ok):
                self_ = jnp.logical_and(a == w, b == n)
                go = jnp.logical_not(self_)
                if ok is not None:
                    go = jnp.logical_and(go, ok)

                @pl.when(go)
                def _():
                    copy = pooled_copy(a, which, b)
                    if start:
                        copy.start()
                    else:
                        copy.wait_send()

                if start:
                    mine = self_ if ok is None else jnp.logical_and(self_, ok)

                    @pl.when(mine)
                    def _():
                        local_copy().start()

                return carry

            lax.fori_loop(0, nw, step, 0)

    each_target(True)
    pack(lambda y: hidden[y], edge2)
    second = fine_copies(hidden.at[0], hidden.at[fy - 1], edge2, halo2, side2, hsend, hrecv)
    send(second)
    clear(second)

    short_bands(k3, wc, cz + 2, 0, cc)
    short_bands(k3, wq, cz + 2, cc, cf)
    short_bands(k4, wm, cz, 0, cc)
    receive(cmade)

    def spread(field, raw, y, height):
        row = raw.astype(F32)
        spot = lanes(row.shape)
        cols = pl.ds(y * cx, cx)
        field[pl.ds(height, raw.shape[0]), cols] = raw
        field[pl.ds(0, raw.shape[0]), cols] = jnp.where(
            spot == 0, 0.0, pltpu.roll(row, 1, 1)).astype(BF16)
        field[pl.ds(2 * height, raw.shape[0]), cols] = jnp.where(
            spot == cx - 1, 0.0, pltpu.roll(row, cx - 1, 1)).astype(BF16)

    for y in range(cy + 4):
        spread(xc3, cbuf[y], y, (cz + 4) * cc)
    high = wq.shape[2] // 3
    if high > tall:
        for dx in range(3):
            xp3[pl.ds(dx * high + tall, high - tall), :] = jnp.zeros(
                (high - tall, xp3.shape[1]), BF16)
    lowl = lax.broadcasted_iota(jnp.int32, (cx, 4 * cx), 0)
    wide_ = lanes((cx, 4 * cx))
    settle = []
    for m in range(nn):
        goal = lowl // xs * cx + m * xs + lowl % xs
        settle.append(jnp.where(goal == wide_, 1.0, 0.0).astype(BF16))
    for k in range(reach + 2):
        tile = n * reach + k - 1
        ok = jnp.logical_and(tile >= 0, tile < nw)

        @pl.when(ok)
        def _(k=k):
            total = None
            for m in range(nn):
                pltpu.make_async_copy(pool.at[pl.ds(0, half)], prcv.at[k, m], precv.at[k, m]).wait()
                term = dot(prcv[k, m], settle[m])
                total = term if total is None else total + term
            for j in range(2):
                even = total[:, j * cx:(j + 1) * cx]
                odd = total[:, (2 + j) * cx:(3 + j) * cx]
                parts = []
                for z in range(half // cf):
                    parts += [even[z * cf:(z + 1) * cf], odd[z * cf:(z + 1) * cf]]
                spread(xp3, jnp.concatenate(parts, axis=0).astype(BF16), 2 * k + j, high)

        @pl.when(jnp.logical_not(ok))
        def _(k=k):
            for dx in range(3):
                xp3[pl.ds(dx * high, tall), pl.ds(2 * k * cx, 2 * cx)] = jnp.zeros(
                    (tall, 2 * cx), BF16)

    mids = (cz + 2) * cc
    zrow = lax.broadcasted_iota(jnp.int32, (mids, 1), 0) // cc + (w * cz - 1)
    zok = jnp.logical_and(zrow >= 0, zrow < nw * cz)
    for h in range((cy + 2) // 2):
        both = conv(wc, xc3, 2 * h * cx, 2 * cx) + conv(wq, xp3, 2 * h * cx, 2 * cx)
        both = jnp.maximum(both + bc1, 0.0)
        ypos = lanes((mids, 2 * cx)) // cx + (n * cy - 1 + 2 * h)
        yok = jnp.logical_and(ypos >= 0, ypos < nn * cy)
        both = jnp.where(jnp.logical_and(zok, yok), both, 0.0).astype(BF16)
        for j in range(2):
            spread(x3m, both[:, j * cx:(j + 1) * cx], 2 * h + j, mids)
    for h in range(cy // 2):
        both = jnp.maximum(conv(wm, x3m, 2 * h * cx, 2 * cx) + bc2, 0.0).astype(BF16)
        near = jnp.concatenate(
            [dot(wp[...], both[z * cc:(z + 1) * cc]) for z in range(cz)], axis=0)
        group = lanes((cf, cx)) // xs
        for m in range(nn):
            total = jnp.zeros((cf, cx), F32)
            for j in range(2):
                for z in range(cz):
                    piece = near[z * cf:(z + 1) * cf, j * cx:(j + 1) * cx]
                    spot = j * cz + z
                    turn = (spot - m) * xs % cx
                    piece = pltpu.roll(piece, turn, 1) if turn else piece
                    total = jnp.where(group == spot, piece, total)
            ctx[h, m] = total.astype(BF16)
        for j in range(2):
            cout[2 * h + j] = both[:, j * cx:(j + 1) * cx]

    def context_step(start):
        def step(i, carry):
            k, m = i // nn, i % nn
            self_ = jnp.logical_and(n * reach + k == w, m == n)

            @pl.when(jnp.logical_not(self_))
            def _():
                copy = remote(ctx.at[k, m], crcv.at[w], tsend.at[k, m], trecv.at[w],
                              n * reach + k, m)
                if start:
                    copy.start()
                else:
                    copy.wait_send()

            if start:
                @pl.when(self_)
                def _():
                    pltpu.make_async_copy(ctx.at[k, m], crcv.at[w], trecv.at[w]).start()

            return carry

        lax.fori_loop(0, reach * nn, step, 0)

    context_step(True)
    bands(k2)
    receive(second)
    expand(lambda y: hidden[y], halo2, side2)
    for a in range(nw):
        pltpu.make_async_copy(ctx.at[0, 0], crcv.at[a], trecv.at[a]).wait()
    near = jnp.concatenate([crcv[a] for a in range(nw)], axis=0)
    for g in range(fy // 4):
        grown = []
        for z in range(cz):
            grow = jnp.where(source == target // 4 + (g * cz + z) * xs, 1.0, 0.0)
            grown.append(dot(near, grow.astype(BF16)))
        parts = []
        for a in range(nw):
            parts += [one[a * cf:(a + 1) * cf] for one in grown]
        more = jnp.concatenate(parts, axis=0) + b2
        for h in range(2):
            y = g * 4 + h * 2
            both = conv(band, x3, y * cx, 2 * cx)
            for k in range(2):
                out[y + k] = (both[:, k * cx:(k + 1) * cx] + more).astype(BF16)

    sent(first)
    sent(cmade)
    sent(second)
    each_target(False)
    context_step(False)


def local(fine_in, coarse_in, w1, b1, w2, b2, wc1, bc1, wc2, bc2, w_proj):
    nw, nn = lax.axis_size("wide"), lax.axis_size("narrow")
    cf, depth, fy, fx = fine_in.shape
    cc, cz, cy, cx = coarse_in.shape
    xs = fx // 4
    rows, crow, reach = depth * cf, cz * cc, cy // 2
    fine = fine_in.transpose(2, 1, 0, 3).reshape(fy, rows, fx)
    coarse = coarse_in.transpose(2, 1, 0, 3).reshape(cy, crow, cx)

    def flat(kernel):
        o, i = kernel.shape[:2]
        return kernel.transpose(2, 3, 4, 0, 1).reshape(27, o, i)

    high = -(-(cz + 4) * cf // 128) * 128
    mids = (cz + 2) * cc
    tall = (cz + 4) * cf
    args = (
        fine, coarse, flat(w1), flat(w2), flat(wc1), flat(wc2),
        b1[None], b2[None], bc1[None], bc2[None], w_proj,
    )
    dims = (nw, nn, depth, cf, cc, fy, cz, cy, cx, xs)
    dma = pltpu.SemaphoreType.DMA
    vmem = pltpu.VMEM
    out, cout = pl.pallas_call(
        functools.partial(kernel, dims),
        name="unet",
        out_shape=(
            jax.ShapeDtypeStruct((fy, rows, fx), BF16),
            jax.ShapeDtypeStruct((cy, crow, cx), BF16),
        ),
        in_specs=[pl.BlockSpec(memory_space=pltpu.VMEM)] * len(args),
        out_specs=(pl.BlockSpec(memory_space=pltpu.VMEM),) * 2,
        scratch_shapes=[
            vmem((2, rows, cx), BF16), vmem((2 * fy, rows), BF16), vmem((6, 2 * fy, rows), BF16),
            vmem((2, rows, cx), BF16), vmem((2 * fy, rows), BF16), vmem((6, 2 * fy, rows), BF16),
            vmem((3, rows, 3 * rows), BF16), vmem((3 * rows, (fy + 2) * cx), BF16),
            vmem((fy, rows, cx), BF16),
            vmem((cy + 4, 3 * crow, cx), BF16), vmem((rows // 2 + 2 * cf, cx), BF16),
            vmem((reach + 2, nn, tall // 2, cx), BF16),
            vmem((3 * 3 * crow, (cy + 4) * cx), BF16), vmem((3 * high, (cy + 4) * cx), BF16),
            vmem((3, mids, 9 * crow), BF16), vmem((3, mids, 3 * high), BF16),
            vmem((3 * mids, (cy + 2) * cx), BF16), vmem((3, crow, 3 * mids), BF16),
            vmem((reach, nn, cf, cx), BF16), vmem((nw, cf, cx), BF16),
            dma((8,)), dma((8,)), dma((8,)), dma((8,)), dma((8,)), dma((8,)),
            dma((3, nw)), dma((reach + 2, nn)), dma((reach, nn)), dma((nw,)), dma,
        ],
        compiler_params=pltpu.CompilerParams(
            collective_id=0, has_side_effects=True, vmem_limit_bytes=63 << 20),
    )(*args)
    fine_out = out.reshape(fy, depth, cf, fx).transpose(2, 1, 0, 3)
    coarse_out = cout.reshape(cy, cz, cc, cx).transpose(2, 1, 0, 3)
    return fine_out, coarse_out


def solution(mesh):
    return jax.shard_map(
        local,
        mesh=mesh,
        in_specs=(
            P(None, None, "wide", "narrow"),
            P(None, "wide", "narrow", None),
        ) + (P(),) * 9,
        out_specs=(P(None, None, "wide", "narrow"), P(None, "wide", "narrow", None)),
        check_vma=False,
    )
```

```python
import functools

import jax
import jax.numpy as jnp
from jax import lax
from jax.experimental import pallas as pl
from jax.experimental.pallas import tpu as pltpu
from jax.sharding import PartitionSpec as P

F32, BF16 = jnp.float32, jnp.bfloat16


def dot(a, b):
    return jnp.dot(a, b, preferred_element_type=F32)


def lanes(shape):
    return lax.broadcasted_iota(jnp.int32, shape, len(shape) - 1)


def kernel(
    dims,
    fine_in, coarse_in, k1, k2, k3, k4, b1_, b2_, bc1_, bc2_, wp,
    out, cout,
    fine, coarse, partial, held,
    halo1, edge1, side1, halo2, edge2, side2, band, x3, hidden,
    cbuf, pool, prcv, xc3, xp3, wc, wq, x3m, wm, ctx, crcv,
    fsend, frecv, hsend, hrecv, csend, crecv, psend, precv, tsend, trecv, lsem,
):
    nw, nn, depth, cf, cc, fy, cz, cy, cx, xs = dims
    rows, crow = depth * cf, cz * cc
    reach = cy // 2
    w, n = lax.axis_index("wide"), lax.axis_index("narrow")

    def at(a, b):
        return {"wide": a, "narrow": b}

    barrier = pltpu.get_barrier_semaphore()

    def greet(i, carry):
        a, b = i // nn, i % nn

        @pl.when(jnp.logical_or(a != w, b != n))
        def _():
            pl.semaphore_signal(barrier, inc=1, device_id=at(a, b))

        return carry

    lax.fori_loop(0, nw * nn, greet, 0)

    def remote(src, dst, ssem, rsem, a, b):
        return pltpu.make_async_remote_copy(
            src_ref=src, dst_ref=dst, send_sem=ssem, recv_sem=rsem,
            device_id=at(a, b), device_id_type=pl.DeviceIdType.MESH)

    def inside(a, b):
        ok_a = jnp.logical_and(a >= 0, a < nw)
        ok_b = jnp.logical_and(b >= 0, b < nn)
        return jnp.logical_and(ok_a, ok_b)

    lane = lanes((rows, cx))
    for z in range(depth):
        fine[:, pl.ds(z * cf, cf), :] = jnp.swapaxes(fine_in[:, z].astype(F32), 0, 1).astype(BF16)
    for z in range(cz):
        coarse[:, pl.ds(z * cc, cc), :] = jnp.swapaxes(
            coarse_in[:, z].astype(F32), 0, 1).astype(BF16)

    def column(bias, copies):
        size = bias.shape[1]
        square = jnp.broadcast_to(bias[...], (size, size))
        diagonal = lax.broadcasted_iota(jnp.int32, (size, size), 0) == lanes((size, size))
        one = jnp.sum(jnp.where(diagonal, square, 0.0), axis=1, keepdims=True)
        return jnp.concatenate([one] * copies, axis=0)

    b1, b2 = column(b1_, depth), column(b2_, depth)
    bc1, bc2 = column(bc1_, cz + 2), column(bc2_, cz)

    def taps(weights, tap, start, size, width, wrap):
        parts = [weights[dz * 9 + tap][:, start:start + size].astype(F32) for dz in range(3)]
        gap = jnp.zeros((parts[0].shape[0], width - 3 * size), F32)
        if wrap:
            return jnp.concatenate([parts[1], parts[2], gap, parts[0]], axis=1)
        return jnp.concatenate(parts + [gap], axis=1)

    def pack(row_of, edge):
        total = jnp.zeros((rows, cx), F32)
        for y in range(fy):
            row = row_of(y).astype(F32)
            first = pltpu.roll(row, y, 1) if y else row
            total = jnp.where(lane == y, first, total)
            last = pltpu.roll(row, fy + 1 + y, 1)
            total = jnp.where(lane == fy + y, last, total)
        edge[...] = total.T[:2 * fy].astype(BF16)

    around = ((-1, 0), (1, 0), (0, -1), (0, 1), (-1, -1), (-1, 1), (1, -1), (1, 1))

    def fine_copies(top, bottom, edge, halo, side, ssem, rsem):
        made = []
        for i, (da, db) in enumerate(around):
            if i == 0:
                src, dst = bottom, halo.at[0]
            elif i == 1:
                src, dst = top, halo.at[1]
            else:
                src, dst = edge, side.at[i - 2]
            made.append((dst, w - da, n - db, w + da, n + db,
                         remote(src, dst, ssem.at[i], rsem.at[i], w - da, n - db)))
        return made

    def send(made):
        for dst, a, b, _, _, copy in made:
            pl.when(inside(a, b))(copy.start)

    def clear(made):
        for dst, _, _, a, b, copy in made:
            @pl.when(jnp.logical_not(inside(a, b)))
            def _(dst=dst):
                dst[...] = jnp.zeros(dst.shape, BF16)

    def receive(made):
        for dst, _, _, a, b, copy in made:
            pl.when(inside(a, b))(copy.wait_recv)

    def sent(made):
        for dst, a, b, _, _, copy in made:
            pl.when(inside(a, b))(copy.wait_send)

    def expand(row_of, halo, side):
        gap = jnp.zeros((cx - 2 * fy, rows), F32)
        left, right, ul, ur, dl, dr = [
            jnp.concatenate([side[i].astype(F32), gap], axis=0).T for i in range(6)]
        for y in range(-1, fy + 1):
            if y < 0:
                raw, lcol, rcol, j = halo[0], ul, ur, fy - 1
            elif y == fy:
                raw, lcol, rcol, j = halo[1], dl, dr, 0
            else:
                raw, lcol, rcol, j = row_of(y), left, right, y
            row = raw.astype(F32)
            cols = pl.ds((y + 1) * cx, cx)
            x3[pl.ds(rows, rows), cols] = raw
            x3[pl.ds(0, rows), cols] = jnp.where(
                lane == 0, pltpu.roll(lcol, cx - fy - j, 1), pltpu.roll(row, 1, 1)).astype(BF16)
            moved = pltpu.roll(rcol, cx - 1 - j, 1)
            x3[pl.ds(2 * rows, rows), cols] = jnp.where(
                lane == cx - 1, moved, pltpu.roll(row, cx - 1, 1)).astype(BF16)

    def bands(base):
        spot = lanes((cf, rows))
        for tap in range(9):
            dy, dx = tap // 3, tap % 3
            piece = taps(base, tap, 0, cf, rows, True)
            for z in range(depth):
                part = pltpu.roll(piece, z * cf, 1) if z else piece
                if z == 0:
                    part = jnp.where(spot >= rows - cf, 0.0, part)
                if z == depth - 1:
                    part = jnp.where(spot < cf, 0.0, part)
                band[dy, pl.ds(z * cf, cf), pl.ds(dx * rows, rows)] = part.astype(BF16)

    def short_bands(base, target, count, start, step):
        size, width = base.shape[1], target.shape[2] // 3
        for tap in range(9):
            dy, dx = tap // 3, tap % 3
            piece = taps(base, tap, start, step, width, False)
            for z in range(count):
                part = pltpu.roll(piece, z * step, 1) if z else piece
                target[dy, pl.ds(z * size, size), pl.ds(dx * width, width)] = part.astype(BF16)

    def conv(weights, field, start, width):
        total = None
        for dy in range(3):
            term = dot(weights[dy], field[:, pl.ds(start + dy * cx, width)])
            total = term if total is None else total + term
        return total

    pack(lambda y: fine[y], edge1)
    first = fine_copies(fine.at[0], fine.at[fy - 1], edge1, halo1, side1, fsend, frecv)
    cmade = []
    for i, (da, db) in enumerate(around):
        zpos = pl.ds((da + 1) * crow, crow)
        if db == 0:
            src, dst = coarse, cbuf.at[pl.ds(2, cy), zpos]
        elif db < 0:
            src, dst = coarse.at[pl.ds(cy - 2, 2)], cbuf.at[pl.ds(0, 2), zpos]
        else:
            src, dst = coarse.at[pl.ds(0, 2)], cbuf.at[pl.ds(cy + 2, 2), zpos]
        cmade.append((dst, w - da, n - db, w + da, n + db,
                      remote(src, dst, csend.at[i], crecv.at[i], w - da, n - db)))
    pl.semaphore_wait(barrier, nw * nn - 1)
    send(first)
    clear(first)
    clear(cmade)
    cbuf[pl.ds(2, cy), pl.ds(crow, crow), :] = coarse[...]
    pool[pl.ds(0, cf), :] = jnp.zeros((cf, cx), BF16)
    pool[pl.ds(cf + rows // 2, cf), :] = jnp.zeros((cf, cx), BF16)
    bands(k1)
    short_bands(k3, wc, cz + 2, 0, cc)
    short_bands(k3, wq, cz + 2, cc, cf)
    short_bands(k4, wm, cz, 0, cc)
    receive(first)
    send(cmade)
    expand(lambda y: fine[y], halo1, side1)

    source = lax.broadcasted_iota(jnp.int32, (cx, cx), 0)
    target = lanes((cx, cx))
    for g in range(fy // 4):
        place = jnp.where(target == source // 4 + g * xs, 1.0, 0.0).astype(BF16)
        total = None
        for h in range(2):
            y = g * 4 + h * 2
            both = jnp.maximum(conv(band, x3, y * cx, 2 * cx) + b1, 0.0).astype(BF16)
            for k in range(2):
                row = both[:, k * cx:(k + 1) * cx]
                hidden[y + k] = row
                term = dot(row, place)
                total = term if total is None else total + term
        if g == 0:
            summed = total
        else:
            summed = summed + total
    mean = summed * (1.0 / 16.0)
    turned = pltpu.roll(mean, cx // 2, 1)
    for z in range(depth // 2):
        first_z = mean[2 * z * cf:(2 * z + 1) * cf]
        pool[pl.ds((z + 1) * cf, cf), :] = (
            first_z + turned[(2 * z + 1) * cf:(2 * z + 2) * cf]).astype(BF16)

    tall = (cz + 4) * cf
    half = tall // 2
    step_z = cz // 2 * cf

    def pooled_copy(a, which, b):
        k = w - b * reach + 1
        return remote(pool.at[pl.ds(pl.multiple_of(a * step_z, cf), half)], prcv.at[k, n],
                      psend.at[which, a], precv.at[k, n], a, b)

    def local_copy():
        k = w - n * reach + 1
        return pltpu.make_async_copy(pool.at[pl.ds(pl.multiple_of(w * step_z, cf), half)],
                                     prcv.at[k, n], precv.at[k, n])

    home = w // reach
    rest = w % reach
    targets = (
        (home, None),
        (home - 1, jnp.logical_and(rest == 0, home >= 1)),
        (home + 1, jnp.logical_and(rest == reach - 1, home + 1 < nn)),
    )

    def each_target(start):
        for which, (b, ok) in enumerate(targets):
            def step(a, carry, which=which, b=b, ok=ok):
                self_ = jnp.logical_and(a == w, b == n)
                go = jnp.logical_not(self_)
                if ok is not None:
                    go = jnp.logical_and(go, ok)

                @pl.when(go)
                def _():
                    copy = pooled_copy(a, which, b)
                    if start:
                        copy.start()
                    else:
                        copy.wait_send()

                if start:
                    mine = self_ if ok is None else jnp.logical_and(self_, ok)

                    @pl.when(mine)
                    def _():
                        local_copy().start()

                return carry

            lax.fori_loop(0, nw, step, 0)

    each_target(True)
    pack(lambda y: hidden[y], edge2)
    second = fine_copies(hidden.at[0], hidden.at[fy - 1], edge2, halo2, side2, hsend, hrecv)
    send(second)
    clear(second)

    receive(cmade)

    def spread(field, raw, y, height):
        row = raw.astype(F32)
        spot = lanes(row.shape)
        cols = pl.ds(y * cx, cx)
        field[pl.ds(height, raw.shape[0]), cols] = raw
        field[pl.ds(0, raw.shape[0]), cols] = jnp.where(
            spot == 0, 0.0, pltpu.roll(row, 1, 1)).astype(BF16)
        field[pl.ds(2 * height, raw.shape[0]), cols] = jnp.where(
            spot == cx - 1, 0.0, pltpu.roll(row, cx - 1, 1)).astype(BF16)

    for y in range(cy + 4):
        spread(xc3, cbuf[y], y, (cz + 4) * cc)
    high = wq.shape[2] // 3
    if high > tall:
        for dx in range(3):
            xp3[pl.ds(dx * high + tall, high - tall), :] = jnp.zeros(
                (high - tall, xp3.shape[1]), BF16)
    for h in range((cy + 2) // 2):
        partial[h] = conv(wc, xc3, 2 * h * cx, 2 * cx)
    lowl = lax.broadcasted_iota(jnp.int32, (cx, 4 * cx), 0)
    wide_ = lanes((cx, 4 * cx))
    settle = []
    for m in range(nn):
        goal = lowl // xs * cx + m * xs + lowl % xs
        settle.append(jnp.where(goal == wide_, 1.0, 0.0).astype(BF16))
    for k in range(reach + 2):
        tile = n * reach + k - 1
        ok = jnp.logical_and(tile >= 0, tile < nw)

        @pl.when(ok)
        def _(k=k):
            total = None
            for m in range(nn):
                pltpu.make_async_copy(pool.at[pl.ds(0, half)], prcv.at[k, m], precv.at[k, m]).wait()
                term = dot(prcv[k, m], settle[m])
                total = term if total is None else total + term
            for j in range(2):
                even = total[:, j * cx:(j + 1) * cx]
                odd = total[:, (2 + j) * cx:(3 + j) * cx]
                parts = []
                for z in range(half // cf):
                    parts += [even[z * cf:(z + 1) * cf], odd[z * cf:(z + 1) * cf]]
                spread(xp3, jnp.concatenate(parts, axis=0).astype(BF16), 2 * k + j, high)

        @pl.when(jnp.logical_not(ok))
        def _(k=k):
            for dx in range(3):
                xp3[pl.ds(dx * high, tall), pl.ds(2 * k * cx, 2 * cx)] = jnp.zeros(
                    (tall, 2 * cx), BF16)

    mids = (cz + 2) * cc
    zrow = lax.broadcasted_iota(jnp.int32, (mids, 1), 0) // cc + (w * cz - 1)
    zok = jnp.logical_and(zrow >= 0, zrow < nw * cz)
    for h in range((cy + 2) // 2):
        both = partial[h] + conv(wq, xp3, 2 * h * cx, 2 * cx)
        both = jnp.maximum(both + bc1, 0.0)
        ypos = lanes((mids, 2 * cx)) // cx + (n * cy - 1 + 2 * h)
        yok = jnp.logical_and(ypos >= 0, ypos < nn * cy)
        both = jnp.where(jnp.logical_and(zok, yok), both, 0.0).astype(BF16)
        for j in range(2):
            spread(x3m, both[:, j * cx:(j + 1) * cx], 2 * h + j, mids)
    for h in range(cy // 2):
        both = jnp.maximum(conv(wm, x3m, 2 * h * cx, 2 * cx) + bc2, 0.0).astype(BF16)
        near = jnp.concatenate(
            [dot(wp[...], both[z * cc:(z + 1) * cc]) for z in range(cz)], axis=0)
        group = lanes((cf, cx)) // xs
        for m in range(nn):
            total = jnp.zeros((cf, cx), F32)
            for j in range(2):
                for z in range(cz):
                    piece = near[z * cf:(z + 1) * cf, j * cx:(j + 1) * cx]
                    spot = j * cz + z
                    turn = (spot - m) * xs % cx
                    piece = pltpu.roll(piece, turn, 1) if turn else piece
                    total = jnp.where(group == spot, piece, total)
            ctx[h, m] = total.astype(BF16)
        for j in range(2):
            cout[2 * h + j] = both[:, j * cx:(j + 1) * cx]

    def context_step(start):
        def step(i, carry):
            k, m = i // nn, i % nn
            self_ = jnp.logical_and(n * reach + k == w, m == n)

            @pl.when(jnp.logical_not(self_))
            def _():
                copy = remote(ctx.at[k, m], crcv.at[w], tsend.at[k, m], trecv.at[w],
                              n * reach + k, m)
                if start:
                    copy.start()
                else:
                    copy.wait_send()

            if start:
                @pl.when(self_)
                def _():
                    pltpu.make_async_copy(ctx.at[k, m], crcv.at[w], trecv.at[w]).start()

            return carry

        lax.fori_loop(0, reach * nn, step, 0)

    context_step(True)
    bands(k2)
    receive(second)
    expand(lambda y: hidden[y], halo2, side2)
    for h in range(fy // 2):
        held[h] = conv(band, x3, 2 * h * cx, 2 * cx)
    for a in range(nw):
        pltpu.make_async_copy(ctx.at[0, 0], crcv.at[a], trecv.at[a]).wait()
    near = jnp.concatenate([crcv[a] for a in range(nw)], axis=0)
    for g in range(fy // 4):
        grown = []
        for z in range(cz):
            grow = jnp.where(source == target // 4 + (g * cz + z) * xs, 1.0, 0.0)
            grown.append(dot(near, grow.astype(BF16)))
        parts = []
        for a in range(nw):
            parts += [one[a * cf:(a + 1) * cf] for one in grown]
        more = jnp.concatenate(parts, axis=0) + b2
        for h in range(2):
            y = g * 4 + h * 2
            both = held[y // 2]
            for k in range(2):
                out[y + k] = (both[:, k * cx:(k + 1) * cx] + more).astype(BF16)

    sent(first)
    sent(cmade)
    sent(second)
    each_target(False)
    context_step(False)


def local(fine_in, coarse_in, w1, b1, w2, b2, wc1, bc1, wc2, bc2, w_proj):
    nw, nn = lax.axis_size("wide"), lax.axis_size("narrow")
    cf, depth, fy, fx = fine_in.shape
    cc, cz, cy, cx = coarse_in.shape
    xs = fx // 4
    rows, crow, reach = depth * cf, cz * cc, cy // 2

    def flat(kernel):
        o, i = kernel.shape[:2]
        return kernel.transpose(2, 3, 4, 0, 1).reshape(27, o, i)

    high = -(-(cz + 4) * cf // 128) * 128
    mids = (cz + 2) * cc
    tall = (cz + 4) * cf
    args = (
        fine_in, coarse_in, flat(w1), flat(w2), flat(wc1), flat(wc2),
        b1[None], b2[None], bc1[None], bc2[None], w_proj,
    )
    dims = (nw, nn, depth, cf, cc, fy, cz, cy, cx, xs)
    dma = pltpu.SemaphoreType.DMA
    vmem = pltpu.VMEM
    out, cout = pl.pallas_call(
        functools.partial(kernel, dims),
        name="unet",
        out_shape=(
            jax.ShapeDtypeStruct((fy, rows, fx), BF16),
            jax.ShapeDtypeStruct((cy, crow, cx), BF16),
        ),
        in_specs=[pl.BlockSpec(memory_space=pltpu.VMEM)] * len(args),
        out_specs=(pl.BlockSpec(memory_space=pltpu.VMEM),) * 2,
        scratch_shapes=[
            vmem((fy, rows, cx), BF16), vmem((cy, crow, cx), BF16),
            vmem(((cy + 2) // 2, mids, 2 * cx), F32), vmem((fy // 2, rows, 2 * cx), F32),
            vmem((2, rows, cx), BF16), vmem((2 * fy, rows), BF16), vmem((6, 2 * fy, rows), BF16),
            vmem((2, rows, cx), BF16), vmem((2 * fy, rows), BF16), vmem((6, 2 * fy, rows), BF16),
            vmem((3, rows, 3 * rows), BF16), vmem((3 * rows, (fy + 2) * cx), BF16),
            vmem((fy, rows, cx), BF16),
            vmem((cy + 4, 3 * crow, cx), BF16), vmem((rows // 2 + 2 * cf, cx), BF16),
            vmem((reach + 2, nn, tall // 2, cx), BF16),
            vmem((3 * 3 * crow, (cy + 4) * cx), BF16), vmem((3 * high, (cy + 4) * cx), BF16),
            vmem((3, mids, 9 * crow), BF16), vmem((3, mids, 3 * high), BF16),
            vmem((3 * mids, (cy + 2) * cx), BF16), vmem((3, crow, 3 * mids), BF16),
            vmem((reach, nn, cf, cx), BF16), vmem((nw, cf, cx), BF16),
            dma((8,)), dma((8,)), dma((8,)), dma((8,)), dma((8,)), dma((8,)),
            dma((3, nw)), dma((reach + 2, nn)), dma((reach, nn)), dma((nw,)), dma,
        ],
        compiler_params=pltpu.CompilerParams(
            collective_id=0, has_side_effects=True, vmem_limit_bytes=63 << 20),
    )(*args)
    fine_out = out.reshape(fy, depth, cf, fx).transpose(2, 1, 0, 3)
    coarse_out = cout.reshape(cy, cz, cc, cx).transpose(2, 1, 0, 3)
    return fine_out, coarse_out


def solution(mesh):
    return jax.shard_map(
        local,
        mesh=mesh,
        in_specs=(
            P(None, None, "wide", "narrow"),
            P(None, "wide", "narrow", None),
        ) + (P(),) * 9,
        out_specs=(P(None, None, "wide", "narrow"), P(None, "wide", "narrow", None)),
        check_vma=False,
    )
```

```python
import functools

import jax
import jax.numpy as jnp
from jax import lax
from jax.experimental import pallas as pl
from jax.experimental.pallas import tpu as pltpu
from jax.sharding import PartitionSpec as P

F32, BF16 = jnp.float32, jnp.bfloat16


def dot(a, b):
    return jnp.dot(a, b, preferred_element_type=F32)


def lanes(shape):
    return lax.broadcasted_iota(jnp.int32, shape, len(shape) - 1)


def kernel(
    dims,
    fine_in, coarse_in, k1, k2, k3, k4, b1_, b2_, bc1_, bc2_, wp,
    out, cout,
    fine, coarse, partial, held,
    halo1, edge1, side1, halo2, edge2, side2, band, x3, hidden,
    cbuf, pool, prcv, xc3, xp3, wc, wq, x3m, wm, ctx, crcv,
    fsend, frecv, hsend, hrecv, csend, crecv, psend, precv, tsend, trecv, lsem,
):
    nw, nn, depth, cf, cc, fy, cz, cy, cx, xs = dims
    rows, crow = depth * cf, cz * cc
    reach = cy // 2
    w, n = lax.axis_index("wide"), lax.axis_index("narrow")

    def at(a, b):
        return {"wide": a, "narrow": b}

    barrier = pltpu.get_barrier_semaphore()

    def greet(i, carry):
        a, b = i // nn, i % nn

        @pl.when(jnp.logical_or(a != w, b != n))
        def _():
            pl.semaphore_signal(barrier, inc=1, device_id=at(a, b))

        return carry

    lax.fori_loop(0, nw * nn, greet, 0)

    def remote(src, dst, ssem, rsem, a, b):
        return pltpu.make_async_remote_copy(
            src_ref=src, dst_ref=dst, send_sem=ssem, recv_sem=rsem,
            device_id=at(a, b), device_id_type=pl.DeviceIdType.MESH)

    def inside(a, b):
        ok_a = jnp.logical_and(a >= 0, a < nw)
        ok_b = jnp.logical_and(b >= 0, b < nn)
        return jnp.logical_and(ok_a, ok_b)

    lane = lanes((rows, cx))
    for z in range(depth):
        fine[:, pl.ds(z * cf, cf), :] = jnp.swapaxes(fine_in[:, z].astype(F32), 0, 1).astype(BF16)
    for z in range(cz):
        coarse[:, pl.ds(z * cc, cc), :] = jnp.swapaxes(
            coarse_in[:, z].astype(F32), 0, 1).astype(BF16)

    def column(bias, copies):
        size = bias.shape[1]
        square = jnp.broadcast_to(bias[...], (size, size))
        diagonal = lax.broadcasted_iota(jnp.int32, (size, size), 0) == lanes((size, size))
        one = jnp.sum(jnp.where(diagonal, square, 0.0), axis=1, keepdims=True)
        return jnp.concatenate([one] * copies, axis=0)

    b1, b2 = column(b1_, depth), column(b2_, depth)
    bc1, bc2 = column(bc1_, cz + 2), column(bc2_, cz)

    def taps(weights, tap, start, size, width, wrap):
        parts = [weights[dz * 9 + tap][:, start:start + size].astype(F32) for dz in range(3)]
        gap = jnp.zeros((parts[0].shape[0], width - 3 * size), F32)
        if wrap:
            return jnp.concatenate([parts[1], parts[2], gap, parts[0]], axis=1)
        return jnp.concatenate(parts + [gap], axis=1)

    def pack(row_of, edge):
        total = jnp.zeros((rows, cx), F32)
        for y in range(fy):
            row = row_of(y).astype(F32)
            first = pltpu.roll(row, y, 1) if y else row
            total = jnp.where(lane == y, first, total)
            last = pltpu.roll(row, fy + 1 + y, 1)
            total = jnp.where(lane == fy + y, last, total)
        edge[...] = total.T[:2 * fy].astype(BF16)

    around = ((-1, 0), (1, 0), (0, -1), (0, 1), (-1, -1), (-1, 1), (1, -1), (1, 1))

    def fine_copies(top, bottom, edge, halo, side, ssem, rsem):
        made = []
        for i, (da, db) in enumerate(around):
            if i == 0:
                src, dst = bottom, halo.at[0]
            elif i == 1:
                src, dst = top, halo.at[1]
            else:
                src, dst = edge, side.at[i - 2]
            made.append((dst, w - da, n - db, w + da, n + db,
                         remote(src, dst, ssem.at[i], rsem.at[i], w - da, n - db)))
        return made

    def send(made):
        for dst, a, b, _, _, copy in made:
            pl.when(inside(a, b))(copy.start)

    def clear(made):
        for dst, _, _, a, b, copy in made:
            @pl.when(jnp.logical_not(inside(a, b)))
            def _(dst=dst):
                dst[...] = jnp.zeros(dst.shape, BF16)

    def receive(made):
        for dst, _, _, a, b, copy in made:
            pl.when(inside(a, b))(copy.wait_recv)

    def sent(made):
        for dst, a, b, _, _, copy in made:
            pl.when(inside(a, b))(copy.wait_send)

    def expand(row_of, halo, side):
        gap = jnp.zeros((cx - 2 * fy, rows), F32)
        left, right, ul, ur, dl, dr = [
            jnp.concatenate([side[i].astype(F32), gap], axis=0).T for i in range(6)]
        for y in range(-1, fy + 1):
            if y < 0:
                raw, lcol, rcol, j = halo[0], ul, ur, fy - 1
            elif y == fy:
                raw, lcol, rcol, j = halo[1], dl, dr, 0
            else:
                raw, lcol, rcol, j = row_of(y), left, right, y
            row = raw.astype(F32)
            cols = pl.ds((y + 1) * cx, cx)
            x3[pl.ds(rows, rows), cols] = raw
            x3[pl.ds(0, rows), cols] = jnp.where(
                lane == 0, pltpu.roll(lcol, cx - fy - j, 1), pltpu.roll(row, 1, 1)).astype(BF16)
            moved = pltpu.roll(rcol, cx - 1 - j, 1)
            x3[pl.ds(2 * rows, rows), cols] = jnp.where(
                lane == cx - 1, moved, pltpu.roll(row, cx - 1, 1)).astype(BF16)

    def bands(base):
        spot = lanes((cf, rows))
        for tap in range(9):
            dy, dx = tap // 3, tap % 3
            piece = taps(base, tap, 0, cf, rows, True)
            for z in range(depth):
                part = pltpu.roll(piece, z * cf, 1) if z else piece
                if z == 0:
                    part = jnp.where(spot >= rows - cf, 0.0, part)
                if z == depth - 1:
                    part = jnp.where(spot < cf, 0.0, part)
                band[dy, pl.ds(z * cf, cf), pl.ds(dx * rows, rows)] = part.astype(BF16)

    def short_bands(base, target, count, start, step):
        size, width = base.shape[1], target.shape[2] // 3
        for tap in range(9):
            dy, dx = tap // 3, tap % 3
            piece = taps(base, tap, start, step, width, False)
            for z in range(count):
                part = pltpu.roll(piece, z * step, 1) if z else piece
                target[dy, pl.ds(z * size, size), pl.ds(dx * width, width)] = part.astype(BF16)

    def conv(weights, field, start, width):
        total = None
        for dy in range(3):
            term = dot(weights[dy], field[:, pl.ds(start + dy * cx, width)])
            total = term if total is None else total + term
        return total

    pack(lambda y: fine[y], edge1)
    first = fine_copies(fine.at[0], fine.at[fy - 1], edge1, halo1, side1, fsend, frecv)
    cmade = []
    for i, (da, db) in enumerate(around):
        zpos = pl.ds((da + 1) * crow, crow)
        if db == 0:
            src, dst = coarse, cbuf.at[pl.ds(2, cy), zpos]
        elif db < 0:
            src, dst = coarse.at[pl.ds(cy - 2, 2)], cbuf.at[pl.ds(0, 2), zpos]
        else:
            src, dst = coarse.at[pl.ds(0, 2)], cbuf.at[pl.ds(cy + 2, 2), zpos]
        cmade.append((dst, w - da, n - db, w + da, n + db,
                      remote(src, dst, csend.at[i], crecv.at[i], w - da, n - db)))
    pl.semaphore_wait(barrier, nw * nn - 1)
    send(first)
    clear(first)
    clear(cmade)
    cbuf[pl.ds(2, cy), pl.ds(crow, crow), :] = coarse[...]
    pool[pl.ds(0, cf), :] = jnp.zeros((cf, cx), BF16)
    pool[pl.ds(cf + rows // 2, cf), :] = jnp.zeros((cf, cx), BF16)
    bands(k1)
    send(cmade)
    short_bands(k3, wc, cz + 2, 0, cc)
    short_bands(k3, wq, cz + 2, cc, cf)
    short_bands(k4, wm, cz, 0, cc)
    receive(first)
    expand(lambda y: fine[y], halo1, side1)

    source = lax.broadcasted_iota(jnp.int32, (cx, cx), 0)
    target = lanes((cx, cx))
    for g in range(fy // 4):
        place = jnp.where(target == source // 4 + g * xs, 1.0, 0.0).astype(BF16)
        total = None
        for h in range(2):
            y = g * 4 + h * 2
            both = jnp.maximum(conv(band, x3, y * cx, 2 * cx) + b1, 0.0).astype(BF16)
            for k in range(2):
                row = both[:, k * cx:(k + 1) * cx]
                hidden[y + k] = row
                term = dot(row, place)
                total = term if total is None else total + term
        if g == 0:
            summed = total
        else:
            summed = summed + total
    mean = summed * (1.0 / 16.0)
    turned = pltpu.roll(mean, cx // 2, 1)
    for z in range(depth // 2):
        first_z = mean[2 * z * cf:(2 * z + 1) * cf]
        pool[pl.ds((z + 1) * cf, cf), :] = (
            first_z + turned[(2 * z + 1) * cf:(2 * z + 2) * cf]).astype(BF16)

    tall = (cz + 4) * cf
    half = tall // 2
    step_z = cz // 2 * cf

    def pooled_copy(a, which, b):
        k = w - b * reach + 1
        return remote(pool.at[pl.ds(pl.multiple_of(a * step_z, cf), half)], prcv.at[k, n],
                      psend.at[which, a], precv.at[k, n], a, b)

    def local_copy():
        k = w - n * reach + 1
        return pltpu.make_async_copy(pool.at[pl.ds(pl.multiple_of(w * step_z, cf), half)],
                                     prcv.at[k, n], precv.at[k, n])

    home = w // reach
    rest = w % reach
    targets = (
        (home, None),
        (home - 1, jnp.logical_and(rest == 0, home >= 1)),
        (home + 1, jnp.logical_and(rest == reach - 1, home + 1 < nn)),
    )

    def each_target(start):
        for which, (b, ok) in enumerate(targets):
            def step(a, carry, which=which, b=b, ok=ok):
                self_ = jnp.logical_and(a == w, b == n)
                go = jnp.logical_not(self_)
                if ok is not None:
                    go = jnp.logical_and(go, ok)

                @pl.when(go)
                def _():
                    copy = pooled_copy(a, which, b)
                    if start:
                        copy.start()
                    else:
                        copy.wait_send()

                if start:
                    mine = self_ if ok is None else jnp.logical_and(self_, ok)

                    @pl.when(mine)
                    def _():
                        local_copy().start()

                return carry

            lax.fori_loop(0, nw, step, 0)

    each_target(True)
    pack(lambda y: hidden[y], edge2)
    second = fine_copies(hidden.at[0], hidden.at[fy - 1], edge2, halo2, side2, hsend, hrecv)
    send(second)
    clear(second)

    receive(cmade)

    def spread(field, raw, y, height):
        row = raw.astype(F32)
        spot = lanes(row.shape)
        cols = pl.ds(y * cx, cx)
        field[pl.ds(height, raw.shape[0]), cols] = raw
        field[pl.ds(0, raw.shape[0]), cols] = jnp.where(
            spot == 0, 0.0, pltpu.roll(row, 1, 1)).astype(BF16)
        field[pl.ds(2 * height, raw.shape[0]), cols] = jnp.where(
            spot == cx - 1, 0.0, pltpu.roll(row, cx - 1, 1)).astype(BF16)

    for y in range(cy + 4):
        spread(xc3, cbuf[y], y, (cz + 4) * cc)
    high = wq.shape[2] // 3
    if high > tall:
        for dx in range(3):
            xp3[pl.ds(dx * high + tall, high - tall), :] = jnp.zeros(
                (high - tall, xp3.shape[1]), BF16)
    for h in range((cy + 2) // 2):
        partial[h] = conv(wc, xc3, 2 * h * cx, 2 * cx)
    lowl = lax.broadcasted_iota(jnp.int32, (cx, 4 * cx), 0)
    wide_ = lanes((cx, 4 * cx))
    settle = []
    for m in range(nn):
        goal = lowl // xs * cx + m * xs + lowl % xs
        settle.append(jnp.where(goal == wide_, 1.0, 0.0).astype(BF16))
    for k in range(reach + 2):
        tile = n * reach + k - 1
        ok = jnp.logical_and(tile >= 0, tile < nw)

        @pl.when(ok)
        def _(k=k):
            total = None
            for m in range(nn):
                pltpu.make_async_copy(pool.at[pl.ds(0, half)], prcv.at[k, m], precv.at[k, m]).wait()
                term = dot(prcv[k, m], settle[m])
                total = term if total is None else total + term
            for j in range(2):
                even = total[:, j * cx:(j + 1) * cx]
                odd = total[:, (2 + j) * cx:(3 + j) * cx]
                parts = []
                for z in range(half // cf):
                    parts += [even[z * cf:(z + 1) * cf], odd[z * cf:(z + 1) * cf]]
                spread(xp3, jnp.concatenate(parts, axis=0).astype(BF16), 2 * k + j, high)

        @pl.when(jnp.logical_not(ok))
        def _(k=k):
            for dx in range(3):
                xp3[pl.ds(dx * high, tall), pl.ds(2 * k * cx, 2 * cx)] = jnp.zeros(
                    (tall, 2 * cx), BF16)

    mids = (cz + 2) * cc
    zrow = lax.broadcasted_iota(jnp.int32, (mids, 1), 0) // cc + (w * cz - 1)
    zok = jnp.logical_and(zrow >= 0, zrow < nw * cz)
    for h in range((cy + 2) // 2):
        both = partial[h] + conv(wq, xp3, 2 * h * cx, 2 * cx)
        both = jnp.maximum(both + bc1, 0.0)
        ypos = lanes((mids, 2 * cx)) // cx + (n * cy - 1 + 2 * h)
        yok = jnp.logical_and(ypos >= 0, ypos < nn * cy)
        both = jnp.where(jnp.logical_and(zok, yok), both, 0.0).astype(BF16)
        for j in range(2):
            spread(x3m, both[:, j * cx:(j + 1) * cx], 2 * h + j, mids)
    for h in range(cy // 2):
        both = jnp.maximum(conv(wm, x3m, 2 * h * cx, 2 * cx) + bc2, 0.0).astype(BF16)
        near = jnp.concatenate(
            [dot(wp[...], both[z * cc:(z + 1) * cc]) for z in range(cz)], axis=0)
        group = lanes((cf, cx)) // xs
        for m in range(nn):
            total = jnp.zeros((cf, cx), F32)
            for j in range(2):
                for z in range(cz):
                    piece = near[z * cf:(z + 1) * cf, j * cx:(j + 1) * cx]
                    spot = j * cz + z
                    turn = (spot - m) * xs % cx
                    piece = pltpu.roll(piece, turn, 1) if turn else piece
                    total = jnp.where(group == spot, piece, total)
            ctx[h, m] = total.astype(BF16)
        for j in range(2):
            cout[2 * h + j] = both[:, j * cx:(j + 1) * cx]

    def context_step(start):
        def step(i, carry):
            k, m = i // nn, i % nn
            self_ = jnp.logical_and(n * reach + k == w, m == n)

            @pl.when(jnp.logical_not(self_))
            def _():
                copy = remote(ctx.at[k, m], crcv.at[w], tsend.at[k, m], trecv.at[w],
                              n * reach + k, m)
                if start:
                    copy.start()
                else:
                    copy.wait_send()

            if start:
                @pl.when(self_)
                def _():
                    pltpu.make_async_copy(ctx.at[k, m], crcv.at[w], trecv.at[w]).start()

            return carry

        lax.fori_loop(0, reach * nn, step, 0)

    context_step(True)
    bands(k2)
    receive(second)
    expand(lambda y: hidden[y], halo2, side2)
    for h in range(fy // 2):
        held[h] = conv(band, x3, 2 * h * cx, 2 * cx)
    for a in range(nw):
        pltpu.make_async_copy(ctx.at[0, 0], crcv.at[a], trecv.at[a]).wait()
    near = jnp.concatenate([crcv[a] for a in range(nw)], axis=0)
    for g in range(fy // 4):
        grown = []
        for z in range(cz):
            grow = jnp.where(source == target // 4 + (g * cz + z) * xs, 1.0, 0.0)
            grown.append(dot(near, grow.astype(BF16)))
        parts = []
        for a in range(nw):
            parts += [one[a * cf:(a + 1) * cf] for one in grown]
        more = jnp.concatenate(parts, axis=0) + b2
        for h in range(2):
            y = g * 4 + h * 2
            both = held[y // 2]
            for k in range(2):
                out[y + k] = (both[:, k * cx:(k + 1) * cx] + more).astype(BF16)

    sent(first)
    sent(cmade)
    sent(second)
    each_target(False)
    context_step(False)


def local(fine_in, coarse_in, w1, b1, w2, b2, wc1, bc1, wc2, bc2, w_proj):
    nw, nn = lax.axis_size("wide"), lax.axis_size("narrow")
    cf, depth, fy, fx = fine_in.shape
    cc, cz, cy, cx = coarse_in.shape
    xs = fx // 4
    rows, crow, reach = depth * cf, cz * cc, cy // 2

    def flat(kernel):
        o, i = kernel.shape[:2]
        return kernel.transpose(2, 3, 4, 0, 1).reshape(27, o, i)

    high = -(-(cz + 4) * cf // 128) * 128
    mids = (cz + 2) * cc
    tall = (cz + 4) * cf
    args = (
        fine_in, coarse_in, flat(w1), flat(w2), flat(wc1), flat(wc2),
        b1[None], b2[None], bc1[None], bc2[None], w_proj,
    )
    dims = (nw, nn, depth, cf, cc, fy, cz, cy, cx, xs)
    dma = pltpu.SemaphoreType.DMA
    vmem = pltpu.VMEM
    out, cout = pl.pallas_call(
        functools.partial(kernel, dims),
        name="unet",
        out_shape=(
            jax.ShapeDtypeStruct((fy, rows, fx), BF16),
            jax.ShapeDtypeStruct((cy, crow, cx), BF16),
        ),
        in_specs=[pl.BlockSpec(memory_space=pltpu.VMEM)] * len(args),
        out_specs=(pl.BlockSpec(memory_space=pltpu.VMEM),) * 2,
        scratch_shapes=[
            vmem((fy, rows, cx), BF16), vmem((cy, crow, cx), BF16),
            vmem(((cy + 2) // 2, mids, 2 * cx), F32), vmem((fy // 2, rows, 2 * cx), F32),
            vmem((2, rows, cx), BF16), vmem((2 * fy, rows), BF16), vmem((6, 2 * fy, rows), BF16),
            vmem((2, rows, cx), BF16), vmem((2 * fy, rows), BF16), vmem((6, 2 * fy, rows), BF16),
            vmem((3, rows, 3 * rows), BF16), vmem((3 * rows, (fy + 2) * cx), BF16),
            vmem((fy, rows, cx), BF16),
            vmem((cy + 4, 3 * crow, cx), BF16), vmem((rows // 2 + 2 * cf, cx), BF16),
            vmem((reach + 2, nn, tall // 2, cx), BF16),
            vmem((3 * 3 * crow, (cy + 4) * cx), BF16), vmem((3 * high, (cy + 4) * cx), BF16),
            vmem((3, mids, 9 * crow), BF16), vmem((3, mids, 3 * high), BF16),
            vmem((3 * mids, (cy + 2) * cx), BF16), vmem((3, crow, 3 * mids), BF16),
            vmem((reach, nn, cf, cx), BF16), vmem((nw, cf, cx), BF16),
            dma((8,)), dma((8,)), dma((8,)), dma((8,)), dma((8,)), dma((8,)),
            dma((3, nw)), dma((reach + 2, nn)), dma((reach, nn)), dma((nw,)), dma,
        ],
        compiler_params=pltpu.CompilerParams(
            collective_id=0, has_side_effects=True, vmem_limit_bytes=63 << 20),
    )(*args)
    fine_out = out.reshape(fy, depth, cf, fx).transpose(2, 1, 0, 3)
    coarse_out = cout.reshape(cy, cz, cc, cx).transpose(2, 1, 0, 3)
    return fine_out, coarse_out


def solution(mesh):
    return jax.shard_map(
        local,
        mesh=mesh,
        in_specs=(
            P(None, None, "wide", "narrow"),
            P(None, "wide", "narrow", None),
        ) + (P(),) * 9,
        out_specs=(P(None, None, "wide", "narrow"), P(None, "wide", "narrow", None)),
        check_vma=False,
    )
```
